768 devices in a mesh: dp: 32 (over y, x), tensor: 24 (over z, core).
Axes of the slice: x: 4, y: 8, z: 12, core: 2. Of those that a mesh axis runs over, the one named last changes fastest.
Arguments:
- inputs: float32 [24576, 2048], P(('dp', 'tensor')), parts along dimension 0, may hold values from -6 to 6
- out_grad: float32 [24576, 2048], P(('dp', 'tensor')), parts along dimension 0, may hold values from -6 to 6
- pre_saved: bfloat16 [24576, 9216], P('dp', 'tensor'), parts along dimension 0, may hold values from -6 to 6
- w_in: bfloat16 [2048, 9216], P(None, 'tensor'), may hold values from -0.125 to 0.125
- w_out_t: bfloat16 [2048, 9216], P(None, 'tensor'), may hold values from -0.0625 to 0.0625
Outputs:
- input_grad: float32 [24576, 2048], P(('dp', 'tensor')), parts along dimension 0
- grad_w_in: bfloat16 [65536, 9216], P('dp', 'tensor'), parts along dimension 0
- grad_w_out_t: bfloat16 [65536, 9216], P('dp', 'tensor'), parts along dimension 0
The draws below stay inside these ranges and needn't reach their ends.
There are 32 independent parts, one for each index of `dp`. The reference program is written for one: setup_inputs(seed, part) draws one part's arguments, and reference() takes and returns one part's arrays. A program takes and returns all parts, laid end to end along the dimension named above; an argument that names none is the same for every part. Nothing has to cross between parts.
All inputs are finite; a program needn't handle non-finite values.
Results may differ from the reference program's by a relative error of at most 0.02.
Values may be sent and summed in bfloat16 or wider, within the bound.
A program may use at most 64 MiB of HBM per device.

```python
import jax
import jax.numpy as jnp
from jax import lax

D = 2048
FF_DEV = 384
FF = 9216
ROWS = 768
N_TENSOR = 24


def block_scale(own_key, dims, pieces, least, high):
    level = 1.0
    for axis_at, parts in pieces:
        draws = jax.random.uniform(jax.random.fold_in(jax.random.fold_in(own_key, 6), axis_at), (parts,), jnp.float32, least / len(pieces), high / len(pieces))
        level = level * jnp.repeat(jnp.exp(draws), dims[axis_at] // parts).reshape((-1,) + (1,) * (len(dims) - 1 - axis_at))
    return level


def normal_values(key, extent, width, reach, split=(), dtype=jnp.bfloat16):
    result = width * jax.random.normal(key, extent, jnp.float32)
    if split:
        result = result * block_scale(key, extent, split, -0.22, 0.18)
    return jnp.clip(result, -reach, reach).astype(dtype)


def setup_inputs(seed: int = 0, part: int = 0) -> dict:
    keys = jax.random.split(jax.random.key(seed), 6)
    part_splits = jax.random.split(jax.random.fold_in(keys[5], part), 6)
    inputs = normal_values(part_splits[0], (ROWS, D), 1.0, 6.0, ((0, 24),), jnp.float32)
    out_grad = normal_values(part_splits[1], (ROWS, D), 1.0, 6.0, ((0, 24),), jnp.float32)
    pre_saved = normal_values(part_splits[2], (ROWS, FF), 1.0, 6.0, ((1, 24),))
    w_in = normal_values(keys[3], (D, FF), D ** -0.5, 0.125, ((1, 24),))
    w_out_t = normal_values(keys[4], (D, FF), FF ** -0.5, 0.0625, ((1, 24),))
    return dict(inputs=inputs, out_grad=out_grad, pre_saved=pre_saved, w_in=w_in, w_out_t=w_out_t)


def contract_rows(left, right):
    return lax.dot_general(left, right, (((0,), (0,)), ((), ())), preferred_element_type=jnp.float32)


def contract_cols(left, right):
    return lax.dot_general(left, right, (((1,), (1,)), ((), ())), preferred_element_type=jnp.float32)


def reference(inputs, out_grad, pre_saved, w_in, w_out_t):
    inputs_bf = inputs.astype(jnp.bfloat16)
    grad_bf = out_grad.astype(jnp.bfloat16)
    activ = jnp.maximum(pre_saved, jnp.zeros_like(pre_saved))
    grad_w_out_t = contract_rows(grad_bf, activ).astype(jnp.bfloat16)
    back = jnp.dot(grad_bf, w_out_t, preferred_element_type=jnp.float32)
    hid_grad = jnp.where(pre_saved > 0.0, back, 0.0).astype(jnp.bfloat16)
    grad_w_in = contract_rows(inputs_bf, hid_grad).astype(jnp.bfloat16)
    hid_blocks = hid_grad.reshape(hid_grad.shape[0], N_TENSOR, FF_DEV).transpose(1, 0, 2)
    weight_blocks = w_in.reshape(w_in.shape[0], N_TENSOR, FF_DEV).transpose(1, 0, 2)

    def add_block(total, pair):
        partial_value = contract_cols(pair[0], pair[1]).astype(jnp.bfloat16)
        partial_value = lax.optimization_barrier(partial_value)
        return total + partial_value.astype(jnp.float32), None

    start = jnp.zeros((hid_grad.shape[0], w_in.shape[0]), jnp.float32)
    input_grad, unused = lax.scan(add_block, start, (hid_blocks, weight_blocks))
    return input_grad, grad_w_in, grad_w_out_t
```

```python
import jax
import jax.numpy as jnp
from jax import lax
from jax.experimental import pallas as pl
from jax.experimental.pallas import tpu as pltpu
from jax.sharding import PartitionSpec as P

MESH = pl.DeviceIdType.MESH
CHIPS = 12
TENSOR = 24
ROWS = 32
HALF = 16
D = 2048
FF = 384
TILE = 256
F32 = jnp.float32
BF16 = jnp.bfloat16


def kernel(
    inputs_hbm, grad_hbm, pre_hbm, win_hbm, wout_hbm,
    ig_hbm, gwi_hbm, gwo_hbm,
    stage_x, stage_g, xall, gall, pre, act, hid, win, wout,
    pown, outbox, inbox, rsend, rrecv, igv, gwi, gwo,
    load_sem, store_sem,
    g_send, g_recv, gp_send, gp_recv,
    x_send, x_recv, xp_send, xp_recv,
    b_send, b_recv, r_send, r_recv,
):
    me = lax.axis_index("tensor")
    z = me // 2
    c = lax.rem(me, 2)
    peer = me + 1 - 2 * c
    right = lax.rem(me + 2, TENSOR)
    left = lax.rem(me + TENSOR - 2, TENSOR)

    barrier = pltpu.get_barrier_semaphore()
    for other in (left, right, peer):
        pl.semaphore_signal(barrier, inc=1, device_id={"tensor": other}, device_id_type=MESH)

    loads = [
        pltpu.make_async_copy(src, dst, load_sem.at[i])
        for i, (src, dst) in enumerate((
            (grad_hbm, stage_g), (inputs_hbm, stage_x), (wout_hbm, wout), (pre_hbm, pre), (win_hbm, win),
        ))
    ]
    for load in loads:
        load.start()

    def chip(offset):
        return lax.rem(z + offset + CHIPS, CHIPS)

    def ring(buf, sends, recvs, owner, way, step, half):
        part = buf.at[owner, pl.ds(half * HALF, HALF)]
        return pltpu.make_async_remote_copy(
            src_ref=part, dst_ref=part, send_sem=sends.at[way, step, half], recv_sem=recvs.at[way, step, half],
            device_id={"tensor": left if way else right}, device_id_type=MESH,
        )

    def across(buf, sends, recvs, owner, way, step, half):
        part = buf.at[owner, pl.ds(half * HALF, HALF)]
        return pltpu.make_async_remote_copy(
            src_ref=part, dst_ref=part, send_sem=sends.at[way, step, half], recv_sem=recvs.at[way, step, half],
            device_id={"tensor": peer}, device_id_type=MESH,
        )

    def source(way, step):
        return chip(step) if way else chip(-step)

    def relay(buf, ring_sems, peer_sems, step, half, way, last):
        owner = 2 * source(way, step) + c
        ring(buf, *ring_sems, owner, way, step, half).wait_recv()
        if last is None:
            ring(buf, *ring_sems, owner, way, step + 1, half).start()
        elif last is not True:
            @pl.when(last)
            def _():
                ring(buf, *ring_sems, owner, way, step + 1, half).start()
        across(buf, *peer_sems, owner, way, step, half).start()

    def from_peer(buf, peer_sems, step, half, way):
        owner = 2 * source(way, step) + 1 - c
        across(buf, *peer_sems, owner, way, step, half).wait_recv()

    def begin(buf, ring_sems, peer_sems):
        for half in (0, 1):
            for way in (0, 1):
                ring(buf, *ring_sems, me, way, 1, half).start()
        for half in (0, 1):
            across(buf, *peer_sems, me, 0, 0, half).start()

    g_ring, g_peer = (g_send, g_recv), (gp_send, gp_recv)
    x_ring, x_peer = (x_send, x_recv), (xp_send, xp_recv)

    def box(slot):
        return pltpu.make_async_remote_copy(
            src_ref=outbox.at[slot], dst_ref=inbox.at[slot], send_sem=b_send.at[slot], recv_sem=b_recv.at[slot],
            device_id={"tensor": peer}, device_id_type=MESH,
        )

    def compute(chips, slots):
        owners = []
        for d in chips:
            owners += [2 * d + c, 2 * d + 1 - c]
        lhs = jnp.concatenate([gall[o] for o in owners], axis=0)
        back = jnp.dot(lhs, wout[...], preferred_element_type=F32)
        rows_pre = jnp.concatenate([pre[o] for o in owners], axis=0)
        rows_hid = jnp.where(rows_pre > 0.0, back, 0.0).astype(BF16)
        for i, o in enumerate(owners):
            hid[o] = rows_hid[i * ROWS:(i + 1) * ROWS]

        @pl.loop(0, D // TILE)
        def _(n):
            cols = pl.ds(pl.multiple_of(n * TILE, TILE), TILE)
            part = lax.dot_general(
                rows_hid, win[cols, :], (((1,), (1,)), ((), ())), preferred_element_type=F32
            )
            for i, slot in enumerate(slots):
                pown[slot, :, cols] = part[2 * i * ROWS:(2 * i + 1) * ROWS]
                outbox[slot, :, cols] = part[(2 * i + 1) * ROWS:(2 * i + 2) * ROWS].astype(BF16)
        for slot in slots:
            box(slot).start()

    def slot_of(way, k):
        return k + 6 if way else k

    def rs(way, step):
        if step == 1:
            rows = pl.ds(way * HALF, HALF)
            src, dst = rsend.at[way, step, rows], rrecv.at[way, step, rows]
        else:
            src, dst = rsend.at[way, step], rrecv.at[way, step]
        return pltpu.make_async_remote_copy(
            src_ref=src, dst_ref=dst, send_sem=r_send.at[way, step], recv_sem=r_recv.at[way, step],
            device_id={"tensor": left if way else right}, device_id_type=MESH,
        )

    loads[0].wait()
    gall[me] = stage_g[...].astype(BF16)
    loads[1].wait()
    xall[me] = stage_x[...].astype(BF16)
    pl.semaphore_wait(barrier, 3)

    begin(gall, g_ring, g_peer)
    loads[2].wait()
    loads[3].wait()
    act[...] = jnp.maximum(pre[...], jnp.zeros_like(pre))
    loads[4].wait()
    for half in (0, 1):
        across(gall, *g_peer, 2 * z + 1 - c, 0, 0, half).wait_recv()
    compute([z], [0])

    def gather_step(s, carry):
        for half in (0, 1):
            for way in (0, 1):
                relay(gall, g_ring, g_peer, s, half, way, None if half == way else s < 5)

        @pl.when(s == 5)
        def _():
            begin(xall, x_ring, x_peer)

        @pl.when(s > 1)
        def _():
            for half in (0, 1):
                for way in (0, 1):
                    from_peer(gall, g_peer, s - 1, half, way)
            compute([chip(s - 1), chip(1 - s)], [s - 1, s + 5])
        return carry

    lax.fori_loop(1, 6, gather_step, 0)
    for way in (0, 1):
        relay(gall, g_ring, g_peer, 6, way, way, True)
    for half in (0, 1):
        for way in (0, 1):
            from_peer(gall, g_peer, 5, half, way)
    compute([chip(5), chip(-5)], [5, 11])
    for way in (0, 1):
        from_peer(gall, g_peer, 6, way, way)
    compute([chip(6)], [6])

    def weight_tile(buf, right_ref, out_ref, out_hbm, sem, n):
        cols = pl.ds(pl.multiple_of(n * TILE, TILE), TILE)
        lhs = buf[:, :, cols].reshape(TENSOR * ROWS, TILE)
        rhs = right_ref[...].reshape(TENSOR * ROWS, FF)
        total = lax.dot_general(lhs, rhs, (((0,), (0,)), ((), ())), preferred_element_type=F32)
        out_ref[cols, :] = total.astype(BF16)
        pltpu.make_async_copy(out_ref.at[cols, :], out_hbm.at[cols, :], sem.at[n]).start()

    for step in range(1, 7):
        k = 7 - step
        if step > 1:
            for way in (0, 1):
                rs(way, step - 1).wait_recv()
        if step == 1:
            box(6).wait_recv()
            for way in (0, 1):
                rows = pl.ds(way * HALF, HALF)
                rsend[way, step, rows] = (pown[6, rows] + inbox[6, rows].astype(F32)).astype(BF16)
        else:
            for way in (0, 1):
                slot = slot_of(way, k)
                box(slot).wait_recv()
                if step == 2:
                    rows, rest = pl.ds(way * HALF, HALF), pl.ds((1 - way) * HALF, HALF)
                    rsend[way, step, rows] = (
                        pown[slot, rows] + inbox[slot, rows].astype(F32) + rrecv[way, 1, rows].astype(F32)
                    ).astype(BF16)
                    rsend[way, step, rest] = (pown[slot, rest] + inbox[slot, rest].astype(F32)).astype(BF16)
                else:
                    rsend[way, step] = (
                        pown[slot] + inbox[slot].astype(F32) + rrecv[way, step - 1].astype(F32)
                    ).astype(BF16)
        for way in (0, 1):
            rs(way, step).start()
        for half in (0, 1):
            for way in (0, 1):
                if step < 6:
                    relay(xall, x_ring, x_peer, step, half, way, None if step < 5 or half == way else True)
                elif half == way:
                    relay(xall, x_ring, x_peer, step, half, way, True)
        if step < 5:
            @pl.loop(2 * (step - 1), 2 * step)
            def _(n):
                weight_tile(gall, act, gwo, gwo_hbm, store_sem.at[0], n)

    for half in (0, 1):
        across(xall, *x_peer, 2 * z + 1 - c, 0, 0, half).wait_recv()
    for s in range(1, 7):
        for half in (0, 1):
            for way in (0, 1):
                if s < 6 or half == way:
                    from_peer(xall, x_peer, s, half, way)

    @pl.loop(0, D // TILE)
    def _(n):
        weight_tile(xall, hid, gwi, gwi_hbm, store_sem.at[1], n)

    box(0).wait_recv()
    for way in (0, 1):
        rs(way, 6).wait_recv()
    igv[...] = pown[0] + inbox[0].astype(F32) + rrecv[0, 6].astype(F32) + rrecv[1, 6].astype(F32)
    store = pltpu.make_async_copy(igv, ig_hbm, load_sem.at[0])
    store.start()

    for buf, sends, peers in ((gall, g_ring, g_peer), (xall, x_ring, x_peer)):
        for half in (0, 1):
            across(buf, *peers, me, 0, 0, half).wait_send()
        for s in range(1, 7):
            for half in (0, 1):
                for way in (0, 1):
                    if s < 6 or half == way:
                        ring(buf, *sends, me, way, s, half).wait_send()
                        across(buf, *peers, me, way, s, half).wait_send()
    for slot in range(CHIPS):
        box(slot).wait_send()
    for step in range(1, 7):
        for way in (0, 1):
            rs(way, step).wait_send()

    @pl.loop(0, D // TILE)
    def _(n):
        cols = pl.ds(pl.multiple_of(n * TILE, TILE), TILE)
        pltpu.make_async_copy(gwo.at[cols, :], gwo_hbm.at[cols, :], store_sem.at[0, n]).wait()
        pltpu.make_async_copy(gwi.at[cols, :], gwi_hbm.at[cols, :], store_sem.at[1, n]).wait()
    store.wait()


def on_device(inputs, out_grad, pre_saved, w_in, w_out_t):
    dma = pltpu.SemaphoreType.DMA
    any_spec = pl.BlockSpec(memory_space=pl.ANY)
    return pl.pallas_call(
        kernel,
        out_shape=(
            jax.ShapeDtypeStruct((ROWS, D), F32),
            jax.ShapeDtypeStruct((D, FF), BF16),
            jax.ShapeDtypeStruct((D, FF), BF16),
        ),
        in_specs=[any_spec] * 5,
        out_specs=[any_spec] * 3,
        scratch_shapes=[
            pltpu.VMEM((ROWS, D), F32),
            pltpu.VMEM((ROWS, D), F32),
            pltpu.VMEM((TENSOR, ROWS, D), BF16),
            pltpu.VMEM((TENSOR, ROWS, D), BF16),
            pltpu.VMEM((TENSOR, ROWS, FF), BF16),
            pltpu.VMEM((TENSOR, ROWS, FF), BF16),
            pltpu.VMEM((TENSOR, ROWS, FF), BF16),
            pltpu.VMEM((D, FF), BF16),
            pltpu.VMEM((D, FF), BF16),
            pltpu.VMEM((CHIPS, ROWS, D), F32),
            pltpu.VMEM((CHIPS, ROWS, D), BF16),
            pltpu.VMEM((CHIPS, ROWS, D), BF16),
            pltpu.VMEM((2, 7, ROWS, D), BF16),
            pltpu.VMEM((2, 7, ROWS, D), BF16),
            pltpu.VMEM((ROWS, D), F32),
            pltpu.VMEM((D, FF), BF16),
            pltpu.VMEM((D, FF), BF16),
            dma((5,)), dma((2, D // TILE)),
            dma((2, 7, 2)), dma((2, 7, 2)), dma((2, 7, 2)), dma((2, 7, 2)),
            dma((2, 7, 2)), dma((2, 7, 2)), dma((2, 7, 2)), dma((2, 7, 2)),
            dma((CHIPS,)), dma((CHIPS,)), dma((2, 7)), dma((2, 7)),
        ],
        compiler_params=pltpu.CompilerParams(
            collective_id=0, has_side_effects=True, vmem_limit_bytes=60 * 1024 * 1024
        ),
        cost_estimate=pl.CostEstimate(flops=4_831_838_208, bytes_accessed=8_000_000, transcendentals=0),
        name="expert_backward",
    )(inputs, out_grad, pre_saved.reshape(TENSOR, ROWS, FF), w_in, w_out_t)


def solution(mesh):
    in_specs = (
        P(("dp", "tensor"), None),
        P(("dp", "tensor"), None),
        P("dp", "tensor"),
        P(None, "tensor"),
        P(None, "tensor"),
    )
    out_specs = (P(("dp", "tensor"), None), P("dp", "tensor"), P("dp", "tensor"))
    return jax.shard_map(
        on_device, mesh=mesh, in_specs=in_specs, out_specs=out_specs, check_vma=False
    )
```

```python
import jax
import jax.numpy as jnp
from jax import lax
from jax.experimental import pallas as pl
from jax.experimental.pallas import tpu as pltpu
from jax.sharding import PartitionSpec as P

MESH = pl.DeviceIdType.MESH
CHIPS = 12
TENSOR = 24
ROWS = 32
HALF = 16
D = 2048
COLS = 1024
FF = 384
TILE = 512
TILES = D // TILE
GRAIN = 256
GRAINS = D // GRAIN
F32 = jnp.float32
BF16 = jnp.bfloat16

LAG = 10
FAR = 20
NEAR = 28


def pieces_of(s):
    return range(4) if s == 6 else range(8)


def message_order():
    gather = [(s, j) for s in range(1, 7) for j in pieces_of(s)]
    reduce = [(1, j) for j in range(4)] + [(2, j) for j in (4, 5, 6, 7, 0, 1, 2, 3)]
    reduce += [(s, j) for s in range(3, 7) for j in (4, 5, 6, 7, 0, 1, 2, 3)]
    todo = {"g": list(gather), "r": reduce, "x": list(gather)}
    slot = {}
    t = 0

    def ready(kind, s, j):
        if kind == "r" and s == 1:
            need, lag = [("g", 6, i) for i in range(4)], FAR
        elif kind == "r" and s == 2 and j > 3:
            need, lag = [("g", 5, i) for i in range(8)], NEAR
        elif s == 1:
            return True
        else:
            need, lag = [(kind, s - 1, j)], LAG
        if kind == "r" and s == 6 and todo["x"]:
            return False
        return all(m in slot and slot[m] + lag <= t for m in need)

    while any(todo.values()):
        for kind in "grx":
            if todo[kind] and ready(kind, *todo[kind][0]):
                slot[(kind,) + todo[kind].pop(0)] = t
                break
        t += 1
    return slot


def kernel(
    inputs_hbm, grad_hbm, pre_hbm, win_hbm, wout_hbm,
    igv, gwi, gwo,
    stage_x, stage_g, xall, gall, pre, act, hid, win, wout,
    pown, outbox, inbox, rsend, rrecv, rlast, acc,
    load_sem,
    g_send, g_recv, gp_send, gp_recv,
    x_send, x_recv, xp_send, xp_recv,
    b_send, b_recv, r_send, r_recv, l_send, l_recv,
):
    me = lax.axis_index("tensor")
    z = me // 2
    c = lax.rem(me, 2)
    sign = 1 - 2 * c
    peer = me + sign
    after = lax.rem(me + 2 * sign + TENSOR, TENSOR)
    before = lax.rem(me - 2 * sign + TENSOR, TENSOR)

    barrier = pltpu.get_barrier_semaphore()
    for other in (after, before, peer):
        pl.semaphore_signal(barrier, inc=1, device_id={"tensor": other}, device_id_type=MESH)

    loads = [
        pltpu.make_async_copy(src, dst, load_sem.at[i])
        for i, (src, dst) in enumerate((
            (grad_hbm, stage_g), (inputs_hbm, stage_x), (wout_hbm, wout), (pre_hbm, pre), (win_hbm, win),
        ))
    ]
    for load in loads:
        load.start()

    def chip(offset):
        return lax.rem(z + offset * sign + CHIPS, CHIPS)

    def owner_of(d, j):
        return 2 * d + (c if j < 4 else 1 - c)

    def part(j):
        return pl.ds(j % 4 // 2 * HALF, HALF), pl.ds(j % 2 * COLS, COLS)

    def part64(j):
        return pl.ds(j // 2 * HALF, HALF), pl.ds(j % 2 * COLS, COLS)

    bufs = {"g": gall, "x": xall}
    ring_sems = {"g": (g_send, g_recv), "x": (x_send, x_recv), "r": (r_send, r_recv)}
    peer_sems = {"g": (gp_send, gp_recv), "x": (xp_send, xp_recv)}

    def ring(kind, s, j, d):
        sends, recvs = ring_sems[kind]
        if kind == "r":
            rows, cols = part64(j)
            src, dst = rsend.at[s, rows, cols], rrecv.at[s, rows, cols]
        else:
            rows, cols = part(j)
            src = dst = bufs[kind].at[owner_of(d, j), rows, cols]
        return pltpu.make_async_remote_copy(
            src_ref=src, dst_ref=dst, send_sem=sends.at[s, j], recv_sem=recvs.at[s, j],
            device_id={"tensor": after}, device_id_type=MESH,
        )

    def to_peer(src, dst, send, recv):
        return pltpu.make_async_remote_copy(
            src_ref=src, dst_ref=dst, send_sem=send, recv_sem=recv, device_id={"tensor": peer}, device_id_type=MESH,
        )

    def across(kind, s, j, owner):
        rows, cols = part(j)
        piece = bufs[kind].at[owner, rows, cols]
        sends, recvs = peer_sems[kind]
        return to_peer(piece, piece, sends.at[s, j], recvs.at[s, j])

    def across_own(kind, owner):
        piece = bufs[kind].at[owner]
        sends, recvs = peer_sems[kind]
        return to_peer(piece, piece, sends.at[0, 0], recvs.at[0, 0])

    def from_peer(kind, s):
        for j in pieces_of(s):
            across(kind, s, j, 2 * chip(s) + (1 - c if j < 4 else c)).wait_recv()

    def box(k):
        rows = pl.ds(0, ROWS if k in (0, 6) else 2 * ROWS)
        return to_peer(outbox.at[k, rows], inbox.at[k, rows], b_send.at[k], b_recv.at[k])

    def handover():
        rows = pl.ds(ROWS, ROWS)
        return to_peer(rrecv.at[6, rows], rlast, l_send, l_recv)

    def rows_of(k):
        near, far = chip(k), chip(-k)
        if k in (0, 6):
            return [2 * near + c, 2 * near + 1 - c]
        return [2 * near + c, 2 * near + 1 - c, 2 * far + 1 - c, 2 * far + c]

    def hidden(k):
        owners = rows_of(k)
        lhs = jnp.concatenate([gall[o] for o in owners], axis=0)
        back = jnp.dot(lhs, wout[...], preferred_element_type=F32)
        rows_pre = jnp.concatenate([pre[o] for o in owners], axis=0)
        rows_hid = jnp.where(rows_pre > 0.0, back, 0.0).astype(BF16)
        for i, o in enumerate(owners):
            hid[o] = rows_hid[i * ROWS:(i + 1) * ROWS]

    def share(k, n):
        owners = rows_of(k)
        rows_hid = jnp.concatenate([hid[o] for o in owners], axis=0)
        half = len(owners) // 2 * ROWS
        cols = pl.ds(n * TILE, TILE)
        sums = lax.dot_general(rows_hid, win[cols, :], (((1,), (1,)), ((), ())), preferred_element_type=F32)
        pown[k, :half, cols] = sums[:half]
        outbox[k, :half, cols] = sums[half:].astype(BF16)
        if n == TILES - 1:
            box(k).start()

    def own_rows():
        for load in loads[2:]:
            load.wait()
        hidden(0)

    def near_rows(k):
        from_peer("g", k)
        hidden(k)

    def far_rows():
        from_peer("g", 6)
        hidden(6)
        for n in range(TILES):
            share(6, n)

    def activations():
        act[...] = jnp.maximum(pre[...], jnp.zeros_like(pre))

    def out_tile(n):
        cols = pl.ds(n * GRAIN, GRAIN)
        lhs = gall[:, :, cols].reshape(TENSOR * ROWS, GRAIN)
        rhs = act[...].reshape(TENSOR * ROWS, FF)
        total = lax.dot_general(rhs, lhs, (((0,), (0,)), ((), ())), preferred_element_type=F32)
        gwo[cols, :] = total.T.astype(BF16)

    early = [0, 1, -1, 2, -2, 3, -3, 4]
    late = [-4, 5, -5, 6]

    def in_tile(n, offsets):
        cols = pl.ds(n * GRAIN, GRAIN)
        owners = [o for k in offsets for o in (2 * chip(k) + c, 2 * chip(k) + 1 - c)]
        lhs = jnp.concatenate([xall[o, :, cols] for o in owners], axis=0)
        rhs = jnp.concatenate([hid[o] for o in owners], axis=0)
        total = lax.dot_general(rhs, lhs, (((0,), (0,)), ((), ())), preferred_element_type=F32)
        if offsets is early:
            acc[:, cols] = total
        else:
            gwi[cols, :] = (acc[:, cols] + total).T.astype(BF16)

    def in_tile_early(n):
        in_tile(n, early)

    def in_tile_late(n):
        in_tile(n, late)

    def early_inputs():
        for k in range(1, 5):
            from_peer("x", k)

    def late_inputs():
        for k in (5, 6):
            from_peer("x", k)

    slot = message_order()
    pieces = {}

    def at(when, piece, *args):
        pieces.setdefault(int(when), []).append((piece, args))

    def at_each(when, count, step, piece, *args):
        for n in range(count):
            at(when + n * step, piece, *args, n)

    def arrival(kind, s):
        return max(slot[(kind, s, j)] for j in pieces_of(s)) + LAG

    at(6, own_rows)
    at_each(8, TILES, 1, share, 0)
    at(13, activations)
    for k in range(1, 5):
        at(arrival("g", k) + 3, near_rows, k)
        at_each(arrival("g", k) + 4, TILES, 1, share, k)
    far = arrival("g", 6) + 2
    at(far, far_rows)
    at(far + 1, near_rows, 5)
    at_each(far + 2, TILES, 1, share, 5)
    at_each(far + 10, GRAINS, 2, out_tile)
    begin = max(arrival("x", 4) + 4, far + 10 + 2 * GRAINS)
    at(begin, early_inputs)
    at_each(begin, GRAINS, 1.5, in_tile_early)
    end = max(arrival("x", 6) + 4, begin + int(GRAINS * 1.5))
    at(end, late_inputs)
    at_each(end, GRAINS, 1, in_tile_late)

    boxed = set()

    def mailed(k):
        if k not in boxed:
            boxed.add(k)
            box(k).wait_recv()

    loads[0].wait()
    gall[me] = stage_g[...].astype(BF16)
    pl.semaphore_wait(barrier, 3)
    across_own("g", me).start()

    at_slot = {t: message for message, t in slot.items()}
    last = max(slot.values())
    for t in range(max(last + LAG, *pieces) + 1):
        came = at_slot.get(t - LAG)
        if came is not None:
            kind, s, j = came
            d = chip(-s)
            ring(kind, s, j, d).wait_recv()
            if kind != "r":
                across(kind, s, j, owner_of(d, j)).start()
            elif (s, j) == (6, 7):
                handover().start()
        goes = at_slot.get(t)
        if goes is not None:
            kind, s, j = goes
            if goes == ("x", 1, 0):
                loads[1].wait()
                xall[me] = stage_x[...].astype(BF16)
                across_own("x", me).start()
            if goes in (("g", 1, 4), ("x", 1, 4)):
                across_own(kind, peer).wait_recv()
            if kind == "r":
                k = 7 - s
                mailed(k)
                rows, cols = part64(j)
                total = pown[k, rows, cols] + inbox[k, rows, cols].astype(F32)
                if s > 2 or s == 2 and j < 4:
                    total += rrecv[s - 1, rows, cols].astype(F32)
                rsend[s, rows, cols] = total.astype(BF16)
            ring(kind, s, j, chip(1 - s)).start()
        for piece, args in pieces.get(t, ()):
            piece(*args)

    mailed(0)
    igv[...] = pown[0, :ROWS] + inbox[0, :ROWS].astype(F32) + rrecv[6, :ROWS].astype(F32)
    handover().wait_recv()
    igv[...] += rlast[...].astype(F32)

    for kind in "gx":
        across_own(kind, me).wait_send()
    for kind in "gxr":
        for s in range(1, 7):
            for j in range(8) if kind == "r" and s > 1 else range(4) if kind == "r" else pieces_of(s):
                ring(kind, s, j, z).wait_send()
                if kind != "r":
                    across(kind, s, j, owner_of(z, j)).wait_send()
    for k in range(7):
        box(k).wait_send()
    handover().wait_send()


def write_out(ig, gwi, gwo, ig_hbm, gwi_hbm, gwo_hbm, sem):
    copies = [
        pltpu.make_async_copy(src, dst, sem.at[i])
        for i, (src, dst) in enumerate(((gwi, gwi_hbm), (gwo, gwo_hbm), (ig, ig_hbm)))
    ]
    for copy in copies:
        copy.start()
    for copy in copies:
        copy.wait()


def on_device(inputs, out_grad, pre_saved, w_in, w_out_t):
    dma = pltpu.SemaphoreType.DMA
    any_spec = pl.BlockSpec(memory_space=pl.ANY)
    vmem_spec = pl.BlockSpec(memory_space=pltpu.VMEM)
    shapes = (((ROWS, D), F32), ((D, FF), BF16), ((D, FF), BF16))
    results = pl.pallas_call(
        kernel,
        out_shape=tuple(pltpu.VMEM(*shape) for shape in shapes),
        in_specs=[pl.BlockSpec(memory_space=pltpu.HBM)] * 5,
        out_specs=(vmem_spec,) * 3,
        scratch_shapes=[
            pltpu.VMEM((ROWS, D), F32),
            pltpu.VMEM((ROWS, D), F32),
            pltpu.VMEM((TENSOR, ROWS, D), BF16),
            pltpu.VMEM((TENSOR, ROWS, D), BF16),
            pltpu.VMEM((TENSOR, ROWS, FF), BF16),
            pltpu.VMEM((TENSOR, ROWS, FF), BF16),
            pltpu.VMEM((TENSOR, ROWS, FF), BF16),
            pltpu.VMEM((D, FF), BF16),
            pltpu.VMEM((D, FF), BF16),
            pltpu.VMEM((7, 2 * ROWS, D), F32),
            pltpu.VMEM((7, 2 * ROWS, D), BF16),
            pltpu.VMEM((7, 2 * ROWS, D), BF16),
            pltpu.VMEM((7, 2 * ROWS, D), BF16),
            pltpu.VMEM((7, 2 * ROWS, D), BF16),
            pltpu.VMEM((ROWS, D), BF16),
            pltpu.VMEM((FF, D), F32),
            dma((5,)),
            dma((7, 8)), dma((7, 8)), dma((7, 8)), dma((7, 8)),
            dma((7, 8)), dma((7, 8)), dma((7, 8)), dma((7, 8)),
            dma((7,)), dma((7,)), dma((7, 8)), dma((7, 8)), dma, dma,
        ],
        compiler_params=pltpu.CompilerParams(
            collective_id=0, has_side_effects=True, vmem_limit_bytes=60 * 1024 * 1024
        ),
        cost_estimate=pl.CostEstimate(flops=4_831_838_208, bytes_accessed=8_000_000, transcendentals=0),
        name="expert_backward",
    )(inputs, out_grad, pre_saved.reshape(TENSOR, ROWS, FF), w_in, w_out_t)
    return pl.pallas_call(
        write_out,
        out_shape=tuple(jax.ShapeDtypeStruct(*shape) for shape in shapes),
        in_specs=[any_spec] * 3,
        out_specs=(any_spec,) * 3,
        scratch_shapes=[dma((3,))],
        compiler_params=pltpu.CompilerParams(vmem_limit_bytes=2 * 1024 * 1024),
        name="write_out",
    )(*results)


def solution(mesh):
    in_specs = (
        P(("dp", "tensor"), None),
        P(("dp", "tensor"), None),
        P("dp", "tensor"),
        P(None, "tensor"),
        P(None, "tensor"),
    )
    out_specs = (P(("dp", "tensor"), None), P("dp", "tensor"), P("dp", "tensor"))
    return jax.shard_map(
        on_device, mesh=mesh, in_specs=in_specs, out_specs=out_specs, check_vma=False
    )
```

```python
import jax
import jax.numpy as jnp
from jax import lax
from jax.experimental import pallas as pl
from jax.experimental.pallas import tpu as pltpu
from jax.sharding import PartitionSpec as P

MESH = pl.DeviceIdType.MESH
CHIPS = 12
TENSOR = 24
ROWS = 32
HALF = 16
D = 2048
COLS = 1024
FF = 384
TILE = 512
TILES = D // TILE
GRAIN = 256
GRAINS = D // GRAIN
F32 = jnp.float32
BF16 = jnp.bfloat16

LAG = 10
FAR = 20
NEAR = 30


def pieces_of(s):
    return range(4) if s == 6 else range(8)


def message_order():
    gather = [(s, j) for s in range(1, 7) for j in pieces_of(s)]
    reduce = [(1, j) for j in range(4)] + [(2, j) for j in (4, 5, 6, 7, 0, 1, 2, 3)]
    reduce += [(s, j) for s in range(3, 7) for j in (4, 5, 6, 7, 0, 1, 2, 3)]
    todo = {"g": list(gather), "r": reduce, "x": list(gather)}
    slot = {}
    t = 0

    def ready(kind, s, j):
        if kind == "r" and s == 1:
            need, lag = [("g", 6, i) for i in range(4)], FAR
        elif kind == "r" and s == 2 and j > 3:
            need, lag = [("g", 5, i) for i in range(8)], NEAR
        elif s == 1:
            return kind == "x" or j < 4 or t > 5
        else:
            need, lag = [(kind, s - 1, j)], LAG
        if kind == "r" and s == 6 and todo["x"]:
            return False
        return all(m in slot and slot[m] + lag <= t for m in need)

    while any(todo.values()):
        for kind in "grx":
            if todo[kind] and ready(kind, *todo[kind][0]):
                slot[(kind,) + todo[kind].pop(0)] = t
                break
        t += 1
    return slot


def kernel(
    inputs_hbm, grad_hbm, pre_hbm, win_hbm, wout_hbm,
    igv, gwi, gwo,
    stage_x, stage_g, xall, gall, pre, act, hid, win, wout,
    pown, outbox, inbox, rsend, rrecv, rlast, acc,
    load_sem,
    g_send, g_recv, gp_send, gp_recv,
    x_send, x_recv, xp_send, xp_recv,
    b_send, b_recv, r_send, r_recv, l_send, l_recv,
):
    me = lax.axis_index("tensor")
    z = me // 2
    c = lax.rem(me, 2)
    sign = 1 - 2 * c
    peer = me + sign
    after = lax.rem(me + 2 * sign + TENSOR, TENSOR)
    before = lax.rem(me - 2 * sign + TENSOR, TENSOR)

    barrier = pltpu.get_barrier_semaphore()
    for other in (after, before, peer):
        pl.semaphore_signal(barrier, inc=1, device_id={"tensor": other}, device_id_type=MESH)

    loads = [
        pltpu.make_async_copy(src, dst, load_sem.at[i])
        for i, (src, dst) in enumerate((
            (grad_hbm, stage_g), (inputs_hbm, stage_x), (wout_hbm, wout), (pre_hbm, pre), (win_hbm, win),
        ))
    ]
    loads[0].start()

    def chip(offset):
        return lax.rem(z + offset * sign + CHIPS, CHIPS)

    def owner_of(d, j):
        return 2 * d + (c if j < 4 else 1 - c)

    def part(j):
        return pl.ds(j % 4 // 2 * HALF, HALF), pl.ds(j % 2 * COLS, COLS)

    def part64(j):
        return pl.ds(j // 2 * HALF, HALF), pl.ds(j % 2 * COLS, COLS)

    bufs = {"g": gall, "x": xall}
    ring_sems = {"g": (g_send, g_recv), "x": (x_send, x_recv), "r": (r_send, r_recv)}
    peer_sems = {"g": (gp_send, gp_recv), "x": (xp_send, xp_recv)}

    def ring(kind, s, j, d):
        sends, recvs = ring_sems[kind]
        if kind == "r":
            rows, cols = part64(j)
            src, dst = rsend.at[s, rows, cols], rrecv.at[s, rows, cols]
        else:
            rows, cols = part(j)
            src = dst = bufs[kind].at[owner_of(d, j), rows, cols]
        return pltpu.make_async_remote_copy(
            src_ref=src, dst_ref=dst, send_sem=sends.at[s, j], recv_sem=recvs.at[s, j],
            device_id={"tensor": after}, device_id_type=MESH,
        )

    def to_peer(src, dst, send, recv):
        return pltpu.make_async_remote_copy(
            src_ref=src, dst_ref=dst, send_sem=send, recv_sem=recv, device_id={"tensor": peer}, device_id_type=MESH,
        )

    def across(kind, s, j, owner):
        rows, cols = part(j)
        piece = bufs[kind].at[owner, rows, cols]
        sends, recvs = peer_sems[kind]
        return to_peer(piece, piece, sends.at[s, j], recvs.at[s, j])

    def across_own(kind, owner):
        piece = bufs[kind].at[owner]
        sends, recvs = peer_sems[kind]
        return to_peer(piece, piece, sends.at[0, 0], recvs.at[0, 0])

    def from_peer(kind, s):
        for j in pieces_of(s):
            across(kind, s, j, 2 * chip(s) + (1 - c if j < 4 else c)).wait_recv()

    def box(k):
        rows = pl.ds(0, ROWS if k in (0, 6) else 2 * ROWS)
        return to_peer(outbox.at[k, rows], inbox.at[k, rows], b_send.at[k], b_recv.at[k])

    def handover():
        rows = pl.ds(ROWS, ROWS)
        return to_peer(rrecv.at[6, rows], rlast, l_send, l_recv)

    def rows_of(k):
        near, far = chip(k), chip(-k)
        if k in (0, 6):
            return [2 * near + c, 2 * near + 1 - c]
        return [2 * near + c, 2 * near + 1 - c, 2 * far + 1 - c, 2 * far + c]

    def hidden(k):
        owners = rows_of(k)
        lhs = jnp.concatenate([gall[o] for o in owners], axis=0)
        back = jnp.dot(lhs, wout[...], preferred_element_type=F32)
        rows_pre = jnp.concatenate([pre[o] for o in owners], axis=0)
        rows_hid = jnp.where(rows_pre > 0.0, back, 0.0).astype(BF16)
        for i, o in enumerate(owners):
            hid[o] = rows_hid[i * ROWS:(i + 1) * ROWS]

    def share(k, n):
        owners = rows_of(k)
        rows_hid = jnp.concatenate([hid[o] for o in owners], axis=0)
        half = len(owners) // 2 * ROWS
        cols = pl.ds(n * TILE, TILE)
        sums = lax.dot_general(rows_hid, win[cols, :], (((1,), (1,)), ((), ())), preferred_element_type=F32)
        pown[k, :half, cols] = sums[:half]
        outbox[k, :half, cols] = sums[half:].astype(BF16)
        if n == TILES - 1:
            box(k).start()

    def own_rows():
        for load in loads[2:]:
            load.wait()
        hidden(0)

    def near_rows(k):
        from_peer("g", k)
        hidden(k)

    def far_rows():
        from_peer("g", 6)
        hidden(6)

    def activations():
        act[...] = jnp.maximum(pre[...], jnp.zeros_like(pre))

    def out_tile(n):
        cols = pl.ds(n * GRAIN, GRAIN)
        lhs = gall[:, :, cols].reshape(TENSOR * ROWS, GRAIN)
        rhs = act[...].reshape(TENSOR * ROWS, FF)
        total = lax.dot_general(rhs, lhs, (((0,), (0,)), ((), ())), preferred_element_type=F32)
        gwo[cols, :] = total.T.astype(BF16)

    early = [0, 1, -1, 2, -2, 3, -3, 4]
    late = [-4, 5, -5, 6]

    def in_tile(n, offsets):
        cols = pl.ds(n * GRAIN, GRAIN)
        owners = [o for k in offsets for o in (2 * chip(k) + c, 2 * chip(k) + 1 - c)]
        lhs = jnp.concatenate([xall[o, :, cols] for o in owners], axis=0)
        rhs = jnp.concatenate([hid[o] for o in owners], axis=0)
        total = lax.dot_general(rhs, lhs, (((0,), (0,)), ((), ())), preferred_element_type=F32)
        if offsets is early:
            acc[:, cols] = total
        else:
            gwi[cols, :] = (acc[:, cols] + total).T.astype(BF16)

    def in_tile_early(n):
        in_tile(n, early)

    def in_tile_late(n):
        in_tile(n, late)

    def early_inputs():
        for k in range(1, 5):
            from_peer("x", k)

    def late_inputs():
        for k in (5, 6):
            from_peer("x", k)

    slot = message_order()
    pieces = {}

    def at(when, piece, *args):
        pieces.setdefault(int(when), []).append((piece, args))

    def at_each(when, count, step, piece, *args):
        for n in range(count):
            at(when + n * step, piece, *args, n)

    def arrival(kind, s):
        return max(slot[(kind, s, j)] for j in pieces_of(s)) + LAG

    at(6, own_rows)
    at_each(8, TILES, 1, share, 0)
    at(13, activations)
    for k in range(1, 5):
        at(arrival("g", k) + 3, near_rows, k)
        at_each(arrival("g", k) + 4, TILES, 1, share, k)
    far = arrival("g", 6) + 2
    at(far, far_rows)
    at_each(far + 1, TILES, 1, share, 6)
    at(far + 5, near_rows, 5)
    at_each(far + 6, TILES, 1, share, 5)
    at_each(far + 12, GRAINS, 2, out_tile)
    begin = max(arrival("x", 4) + 4, far + 12 + 2 * GRAINS)
    at(begin, early_inputs)
    at_each(begin, GRAINS, 1.5, in_tile_early)
    end = max(arrival("x", 6) + 4, begin + int(GRAINS * 1.5))
    at(end, late_inputs)
    at_each(end, GRAINS, 0.5, in_tile_late)

    boxed = set()

    def mailed(k):
        if k not in boxed:
            boxed.add(k)
            box(k).wait_recv()

    loads[0].wait()
    for load in loads[1:]:
        load.start()
    gall[me] = stage_g[...].astype(BF16)
    pl.semaphore_wait(barrier, 3)
    across_own("g", me).start()

    at_slot = {t: message for message, t in slot.items()}
    last = max(slot.values())
    for t in range(max(last + LAG, *pieces) + 1):
        came = at_slot.get(t - LAG)
        if came is not None:
            kind, s, j = came
            d = chip(-s)
            ring(kind, s, j, d).wait_recv()
            if kind != "r":
                across(kind, s, j, owner_of(d, j)).start()
            elif (s, j) == (6, 7):
                handover().start()
        goes = at_slot.get(t)
        if goes is not None:
            kind, s, j = goes
            if goes == ("x", 1, 0):
                loads[1].wait()
                xall[me] = stage_x[...].astype(BF16)
                across_own("x", me).start()
            if goes in (("g", 1, 4), ("x", 1, 4)):
                across_own(kind, peer).wait_recv()
            if kind == "r":
                k = 7 - s
                mailed(k)
                rows, cols = part64(j)
                total = pown[k, rows, cols] + inbox[k, rows, cols].astype(F32)
                if s > 2 or s == 2 and j < 4:
                    total += rrecv[s - 1, rows, cols].astype(F32)
                rsend[s, rows, cols] = total.astype(BF16)
            ring(kind, s, j, chip(1 - s)).start()
        for piece, args in pieces.get(t, ()):
            piece(*args)

    mailed(0)
    igv[...] = pown[0, :ROWS] + inbox[0, :ROWS].astype(F32) + rrecv[6, :ROWS].astype(F32)
    handover().wait_recv()
    igv[...] += rlast[...].astype(F32)

    for kind in "gx":
        across_own(kind, me).wait_send()
    for kind in "gxr":
        for s in range(1, 7):
            for j in range(8) if kind == "r" and s > 1 else range(4) if kind == "r" else pieces_of(s):
                ring(kind, s, j, z).wait_send()
                if kind != "r":
                    across(kind, s, j, owner_of(z, j)).wait_send()
    for k in range(7):
        box(k).wait_send()
    handover().wait_send()


def write_out(ig, gwi, gwo, ig_hbm, gwi_hbm, gwo_hbm, sem):
    copies = [
        pltpu.make_async_copy(src, dst, sem.at[i])
        for i, (src, dst) in enumerate(((gwi, gwi_hbm), (gwo, gwo_hbm), (ig, ig_hbm)))
    ]
    for copy in copies:
        copy.start()
    for copy in copies:
        copy.wait()


def on_device(inputs, out_grad, pre_saved, w_in, w_out_t):
    dma = pltpu.SemaphoreType.DMA
    any_spec = pl.BlockSpec(memory_space=pl.ANY)
    vmem_spec = pl.BlockSpec(memory_space=pltpu.VMEM)
    shapes = (((ROWS, D), F32), ((D, FF), BF16), ((D, FF), BF16))
    results = pl.pallas_call(
        kernel,
        out_shape=tuple(pltpu.VMEM(*shape) for shape in shapes),
        in_specs=[pl.BlockSpec(memory_space=pltpu.HBM)] * 5,
        out_specs=(vmem_spec,) * 3,
        scratch_shapes=[
            pltpu.VMEM((ROWS, D), F32),
            pltpu.VMEM((ROWS, D), F32),
            pltpu.VMEM((TENSOR, ROWS, D), BF16),
            pltpu.VMEM((TENSOR, ROWS, D), BF16),
            pltpu.VMEM((TENSOR, ROWS, FF), BF16),
            pltpu.VMEM((TENSOR, ROWS, FF), BF16),
            pltpu.VMEM((TENSOR, ROWS, FF), BF16),
            pltpu.VMEM((D, FF), BF16),
            pltpu.VMEM((D, FF), BF16),
            pltpu.VMEM((7, 2 * ROWS, D), F32),
            pltpu.VMEM((7, 2 * ROWS, D), BF16),
            pltpu.VMEM((7, 2 * ROWS, D), BF16),
            pltpu.VMEM((7, 2 * ROWS, D), BF16),
            pltpu.VMEM((7, 2 * ROWS, D), BF16),
            pltpu.VMEM((ROWS, D), BF16),
            pltpu.VMEM((FF, D), F32),
            dma((5,)),
            dma((7, 8)), dma((7, 8)), dma((7, 8)), dma((7, 8)),
            dma((7, 8)), dma((7, 8)), dma((7, 8)), dma((7, 8)),
            dma((7,)), dma((7,)), dma((7, 8)), dma((7, 8)), dma, dma,
        ],
        compiler_params=pltpu.CompilerParams(
            collective_id=0, has_side_effects=True, vmem_limit_bytes=60 * 1024 * 1024
        ),
        cost_estimate=pl.CostEstimate(flops=4_831_838_208, bytes_accessed=8_000_000, transcendentals=0),
        name="expert_backward",
    )(inputs, out_grad, pre_saved.reshape(TENSOR, ROWS, FF), w_in, w_out_t)
    return pl.pallas_call(
        write_out,
        out_shape=tuple(jax.ShapeDtypeStruct(*shape) for shape in shapes),
        in_specs=[any_spec] * 3,
        out_specs=(any_spec,) * 3,
        scratch_shapes=[dma((3,))],
        compiler_params=pltpu.CompilerParams(vmem_limit_bytes=2 * 1024 * 1024),
        name="write_out",
    )(*results)


def solution(mesh):
    in_specs = (
        P(("dp", "tensor"), None),
        P(("dp", "tensor"), None),
        P("dp", "tensor"),
        P(None, "tensor"),
        P(None, "tensor"),
    )
    out_specs = (P(("dp", "tensor"), None), P("dp", "tensor"), P("dp", "tensor"))
    return jax.shard_map(
        on_device, mesh=mesh, in_specs=in_specs, out_specs=out_specs, check_vma=False
    )
```

```python
import jax
import jax.numpy as jnp
from jax import lax
from jax.experimental import pallas as pl
from jax.experimental.pallas import tpu as pltpu
from jax.sharding import PartitionSpec as P

MESH = pl.DeviceIdType.MESH
CHIPS = 12
TENSOR = 24
ROWS = 32
HALF = 16
D = 2048
COLS = 1024
FF = 384
TILE = 512
TILES = D // TILE
GRAIN = 256
GRAINS = D // GRAIN
F32 = jnp.float32
BF16 = jnp.bfloat16

LAG = 10
FAR = 20
NEAR = 30


def pieces_of(s):
    return range(4) if s == 6 else range(8)


def message_order():
    gather = [(s, j) for s in range(1, 7) for j in pieces_of(s)]
    reduce = [(1, j) for j in range(4)] + [(2, j) for j in (4, 5, 6, 7, 0, 1, 2, 3)]
    reduce += [(s, j) for s in range(3, 7) for j in (4, 5, 6, 7, 0, 1, 2, 3)]
    todo = {"g": list(gather), "r": reduce, "x": list(gather)}
    slot = {}
    t = 0

    def ready(kind, s, j):
        if kind == "r" and s == 1:
            need, lag = [("g", 6, i) for i in range(4)], FAR
        elif kind == "r" and s == 2 and j > 3:
            need, lag = [("g", 5, i) for i in range(8)], NEAR
        elif s == 1:
            return kind == "x" or j < 4 or t > 5
        else:
            need, lag = [(kind, s - 1, j)], LAG
        if kind == "r" and s == 6 and todo["x"]:
            return False
        return all(m in slot and slot[m] + lag <= t for m in need)

    while any(todo.values()):
        for kind in "grx":
            if todo[kind] and ready(kind, *todo[kind][0]):
                slot[(kind,) + todo[kind].pop(0)] = t
                break
        t += 1
    return slot


def kernel(
    inputs_hbm, grad_hbm, pre_hbm, win_hbm, wout_hbm,
    igv, gwi, gwo,
    stage_x, stage_g, xall, gall, pre, act, hid, win, wout,
    pown, outbox, inbox, rsend, rrecv, rlast, acc,
    load_sem,
    g_send, g_recv, gp_send, gp_recv,
    x_send, x_recv, xp_send, xp_recv,
    b_send, b_recv, r_send, r_recv, l_send, l_recv,
):
    me = lax.axis_index("tensor")
    z = me // 2
    c = lax.rem(me, 2)
    sign = 1 - 2 * c
    peer = me + sign
    after = lax.rem(me + 2 * sign + TENSOR, TENSOR)
    before = lax.rem(me - 2 * sign + TENSOR, TENSOR)

    barrier = pltpu.get_barrier_semaphore()
    for other in (after, before, peer):
        pl.semaphore_signal(barrier, inc=1, device_id={"tensor": other}, device_id_type=MESH)

    loads = [
        pltpu.make_async_copy(src, dst, load_sem.at[i])
        for i, (src, dst) in enumerate((
            (grad_hbm, stage_g), (inputs_hbm, stage_x), (wout_hbm, wout), (pre_hbm, pre), (win_hbm, win),
        ))
    ]
    firsts = [
        pltpu.make_async_copy(grad_hbm.at[rows, :], stage_g.at[rows, :], load_sem.at[sem])
        for sem, rows in ((0, pl.ds(0, HALF)), (5, pl.ds(HALF, HALF)))
    ]
    for load in firsts:
        load.start()

    def chip(offset):
        return lax.rem(z + offset * sign + CHIPS, CHIPS)

    def owner_of(d, j):
        return 2 * d + (c if j < 4 else 1 - c)

    def part(j):
        return pl.ds(j % 4 // 2 * HALF, HALF), pl.ds(j % 2 * COLS, COLS)

    def part64(j):
        return pl.ds(j // 2 * HALF, HALF), pl.ds(j % 2 * COLS, COLS)

    bufs = {"g": gall, "x": xall}
    ring_sems = {"g": (g_send, g_recv), "x": (x_send, x_recv), "r": (r_send, r_recv)}
    peer_sems = {"g": (gp_send, gp_recv), "x": (xp_send, xp_recv)}

    def ring(kind, s, j, d):
        sends, recvs = ring_sems[kind]
        if kind == "r":
            rows, cols = part64(j)
            src, dst = rsend.at[s, rows, cols], rrecv.at[s, rows, cols]
        else:
            rows, cols = part(j)
            src = dst = bufs[kind].at[owner_of(d, j), rows, cols]
        return pltpu.make_async_remote_copy(
            src_ref=src, dst_ref=dst, send_sem=sends.at[s, j], recv_sem=recvs.at[s, j],
            device_id={"tensor": after}, device_id_type=MESH,
        )

    def to_peer(src, dst, send, recv):
        return pltpu.make_async_remote_copy(
            src_ref=src, dst_ref=dst, send_sem=send, recv_sem=recv, device_id={"tensor": peer}, device_id_type=MESH,
        )

    def across(kind, s, j, owner):
        rows, cols = part(j)
        piece = bufs[kind].at[owner, rows, cols]
        sends, recvs = peer_sems[kind]
        return to_peer(piece, piece, sends.at[s, j], recvs.at[s, j])

    def across_own(kind, owner):
        piece = bufs[kind].at[owner]
        sends, recvs = peer_sems[kind]
        return to_peer(piece, piece, sends.at[0, 0], recvs.at[0, 0])

    def from_peer(kind, s):
        for j in pieces_of(s):
            across(kind, s, j, 2 * chip(s) + (1 - c if j < 4 else c)).wait_recv()

    def box(k):
        rows = pl.ds(0, ROWS if k in (0, 6) else 2 * ROWS)
        return to_peer(outbox.at[k, rows], inbox.at[k, rows], b_send.at[k], b_recv.at[k])

    def handover():
        rows = pl.ds(ROWS, ROWS)
        return to_peer(rrecv.at[6, rows], rlast, l_send, l_recv)

    def rows_of(k):
        near, far = chip(k), chip(-k)
        if k in (0, 6):
            return [2 * near + c, 2 * near + 1 - c]
        return [2 * near + c, 2 * near + 1 - c, 2 * far + 1 - c, 2 * far + c]

    def hidden(k):
        owners = rows_of(k)
        lhs = jnp.concatenate([gall[o] for o in owners], axis=0)
        back = jnp.dot(lhs, wout[...], preferred_element_type=F32)
        rows_pre = jnp.concatenate([pre[o] for o in owners], axis=0)
        rows_hid = jnp.where(rows_pre > 0.0, back, 0.0).astype(BF16)
        for i, o in enumerate(owners):
            hid[o] = rows_hid[i * ROWS:(i + 1) * ROWS]

    def share(k, n):
        owners = rows_of(k)
        rows_hid = jnp.concatenate([hid[o] for o in owners], axis=0)
        half = len(owners) // 2 * ROWS
        cols = pl.ds(n * TILE, TILE)
        sums = lax.dot_general(rows_hid, win[cols, :], (((1,), (1,)), ((), ())), preferred_element_type=F32)
        pown[k, :half, cols] = sums[:half]
        outbox[k, :half, cols] = sums[half:].astype(BF16)
        if n == TILES - 1:
            box(k).start()

    def own_rows():
        for load in loads[2:]:
            load.wait()
        hidden(0)

    def near_rows(k):
        from_peer("g", k)
        hidden(k)

    def far_rows():
        from_peer("g", 6)
        hidden(6)

    def activations():
        act[...] = jnp.maximum(pre[...], jnp.zeros_like(pre))

    def out_tile(n):
        cols = pl.ds(n * GRAIN, GRAIN)
        lhs = gall[:, :, cols].reshape(TENSOR * ROWS, GRAIN)
        rhs = act[...].reshape(TENSOR * ROWS, FF)
        total = lax.dot_general(rhs, lhs, (((0,), (0,)), ((), ())), preferred_element_type=F32)
        gwo[cols, :] = total.T.astype(BF16)

    early = [0, 1, -1, 2, -2, 3, -3, 4]
    late = [-4, 5, -5, 6]

    def in_tile(n, offsets):
        cols = pl.ds(n * GRAIN, GRAIN)
        owners = [o for k in offsets for o in (2 * chip(k) + c, 2 * chip(k) + 1 - c)]
        lhs = jnp.concatenate([xall[o, :, cols] for o in owners], axis=0)
        rhs = jnp.concatenate([hid[o] for o in owners], axis=0)
        total = lax.dot_general(rhs, lhs, (((0,), (0,)), ((), ())), preferred_element_type=F32)
        if offsets is early:
            acc[:, cols] = total
        else:
            gwi[cols, :] = (acc[:, cols] + total).T.astype(BF16)

    def in_tile_early(n):
        in_tile(n, early)

    def in_tile_late(n):
        in_tile(n, late)

    def early_inputs():
        for k in range(1, 5):
            from_peer("x", k)

    def late_inputs():
        for k in (5, 6):
            from_peer("x", k)

    slot = message_order()
    pieces = {}

    def at(when, piece, *args):
        pieces.setdefault(int(when), []).append((piece, args))

    def at_each(when, count, step, piece, *args):
        for n in range(count):
            at(when + n * step, piece, *args, n)

    def arrival(kind, s):
        return max(slot[(kind, s, j)] for j in pieces_of(s)) + LAG

    at(6, own_rows)
    at_each(8, TILES, 1, share, 0)
    at(13, activations)
    for k in range(1, 5):
        at(arrival("g", k) + 3, near_rows, k)
        at_each(arrival("g", k) + 4, TILES, 1, share, k)
    far = arrival("g", 6) + 2
    at(far, far_rows)
    at_each(far + 1, TILES, 1, share, 6)
    at(far + 5, near_rows, 5)
    at_each(far + 6, TILES, 1, share, 5)
    at_each(far + 12, GRAINS, 2, out_tile)
    begin = max(arrival("x", 4) + 4, far + 12 + 2 * GRAINS)
    at(begin, early_inputs)
    at_each(begin, GRAINS, 1.5, in_tile_early)
    end = max(arrival("x", 6) + 4, begin + int(GRAINS * 1.5))
    at(end, late_inputs)
    at_each(end, GRAINS, 0.5, in_tile_late)

    boxed = set()

    def mailed(k):
        if k not in boxed:
            boxed.add(k)
            box(k).wait_recv()

    for load in firsts:
        load.wait()
    for load in loads[1:]:
        load.start()
    gall[me] = stage_g[...].astype(BF16)
    pl.semaphore_wait(barrier, 3)
    across_own("g", me).start()

    at_slot = {t: message for message, t in slot.items()}
    last = max(slot.values())
    for t in range(max(last + LAG, *pieces) + 1):
        came = at_slot.get(t - LAG)
        if came is not None:
            kind, s, j = came
            d = chip(-s)
            ring(kind, s, j, d).wait_recv()
            if kind != "r":
                across(kind, s, j, owner_of(d, j)).start()
            elif (s, j) == (6, 7):
                handover().start()
        goes = at_slot.get(t)
        if goes is not None:
            kind, s, j = goes
            if goes == ("x", 1, 0):
                loads[1].wait()
                xall[me] = stage_x[...].astype(BF16)
                across_own("x", me).start()
            if goes in (("g", 1, 4), ("x", 1, 4)):
                across_own(kind, peer).wait_recv()
            if kind == "r":
                k = 7 - s
                mailed(k)
                rows, cols = part64(j)
                total = pown[k, rows, cols] + inbox[k, rows, cols].astype(F32)
                if s > 2 or s == 2 and j < 4:
                    total += rrecv[s - 1, rows, cols].astype(F32)
                rsend[s, rows, cols] = total.astype(BF16)
            ring(kind, s, j, chip(1 - s)).start()
        for piece, args in pieces.get(t, ()):
            piece(*args)

    mailed(0)
    igv[...] = pown[0, :ROWS] + inbox[0, :ROWS].astype(F32) + rrecv[6, :ROWS].astype(F32)
    handover().wait_recv()
    igv[...] += rlast[...].astype(F32)

    for kind in "gx":
        across_own(kind, me).wait_send()
    for kind in "gxr":
        for s in range(1, 7):
            for j in range(8) if kind == "r" and s > 1 else range(4) if kind == "r" else pieces_of(s):
                ring(kind, s, j, z).wait_send()
                if kind != "r":
                    across(kind, s, j, owner_of(z, j)).wait_send()
    for k in range(7):
        box(k).wait_send()
    handover().wait_send()


def write_out(ig, gwi, gwo, ig_hbm, gwi_hbm, gwo_hbm, sem):
    pairs = [(ig, ig_hbm)]
    for n in range(TILES):
        rows = pl.ds(n * TILE, TILE)
        pairs += [(gwi.at[rows, :], gwi_hbm.at[rows, :]), (gwo.at[rows, :], gwo_hbm.at[rows, :])]
    copies = [pltpu.make_async_copy(src, dst, sem.at[i]) for i, (src, dst) in enumerate(pairs)]
    for copy in copies:
        copy.start()
    for copy in copies:
        copy.wait()


def on_device(inputs, out_grad, pre_saved, w_in, w_out_t):
    dma = pltpu.SemaphoreType.DMA
    any_spec = pl.BlockSpec(memory_space=pl.ANY)
    vmem_spec = pl.BlockSpec(memory_space=pltpu.VMEM)
    shapes = (((ROWS, D), F32), ((D, FF), BF16), ((D, FF), BF16))
    results = pl.pallas_call(
        kernel,
        out_shape=tuple(pltpu.VMEM(*shape) for shape in shapes),
        in_specs=[pl.BlockSpec(memory_space=pltpu.HBM)] * 5,
        out_specs=(vmem_spec,) * 3,
        scratch_shapes=[
            pltpu.VMEM((ROWS, D), F32),
            pltpu.VMEM((ROWS, D), F32),
            pltpu.VMEM((TENSOR, ROWS, D), BF16),
            pltpu.VMEM((TENSOR, ROWS, D), BF16),
            pltpu.VMEM((TENSOR, ROWS, FF), BF16),
            pltpu.VMEM((TENSOR, ROWS, FF), BF16),
            pltpu.VMEM((TENSOR, ROWS, FF), BF16),
            pltpu.VMEM((D, FF), BF16),
            pltpu.VMEM((D, FF), BF16),
            pltpu.VMEM((7, 2 * ROWS, D), F32),
            pltpu.VMEM((7, 2 * ROWS, D), BF16),
            pltpu.VMEM((7, 2 * ROWS, D), BF16),
            pltpu.VMEM((7, 2 * ROWS, D), BF16),
            pltpu.VMEM((7, 2 * ROWS, D), BF16),
            pltpu.VMEM((ROWS, D), BF16),
            pltpu.VMEM((FF, D), F32),
            dma((6,)),
            dma((7, 8)), dma((7, 8)), dma((7, 8)), dma((7, 8)),
            dma((7, 8)), dma((7, 8)), dma((7, 8)), dma((7, 8)),
            dma((7,)), dma((7,)), dma((7, 8)), dma((7, 8)), dma, dma,
        ],
        compiler_params=pltpu.CompilerParams(
            collective_id=0, has_side_effects=True, vmem_limit_bytes=60 * 1024 * 1024
        ),
        cost_estimate=pl.CostEstimate(flops=4_831_838_208, bytes_accessed=8_000_000, transcendentals=0),
        name="expert_backward",
    )(inputs, out_grad, pre_saved.reshape(TENSOR, ROWS, FF), w_in, w_out_t)
    return pl.pallas_call(
        write_out,
        out_shape=tuple(jax.ShapeDtypeStruct(*shape) for shape in shapes),
        in_specs=[any_spec] * 3,
        out_specs=(any_spec,) * 3,
        scratch_shapes=[dma((2 * TILES + 1,))],
        compiler_params=pltpu.CompilerParams(vmem_limit_bytes=2 * 1024 * 1024),
        name="write_out",
    )(*results)


def solution(mesh):
    in_specs = (
        P(("dp", "tensor"), None),
        P(("dp", "tensor"), None),
        P("dp", "tensor"),
        P(None, "tensor"),
        P(None, "tensor"),
    )
    out_specs = (P(("dp", "tensor"), None), P("dp", "tensor"), P("dp", "tensor"))
    return jax.shard_map(
        on_device, mesh=mesh, in_specs=in_specs, out_specs=out_specs, check_vma=False
    )
```
